32 devices in a mesh: dev: 32 (over z, y, x, core).
Axes of the slice: x: 2, y: 2, z: 4, core: 2. Of those that a mesh axis runs over, the one named last changes fastest.
Arguments:
- density_rows: bfloat16 [24576, 3840], P('dev')
- center_x: float32 [24576], replicated, may hold values from -0.25 to 1.25
- center_y: float32 [24576], replicated, may hold values from 0 to 1
- center_z: float32 [24576], replicated, may hold values from 0 to 1
- exponent: float32 [24576], replicated, may hold values from 0.5 to 150
- brick_blocks: int32 [32, 8], replicated, may hold values from 0 to 191, as said below
Outputs:
- potential: float32 [32, 4096], P('dev')
- ham_rows: float32 [24576, 3840], P('dev')
The draws below stay inside these ranges and needn't reach their ends.
Inputs may be any that keep to these rules, and one draw needn't show every extreme that they name: `brick_blocks`: brick b belongs to device d = b. Its 8 entries are distinct blocks; 4 of them are owned by one of the devices d - 1, d, d + 1 (cyclically) and 2 by each of the other two, where block I is owned by device I // 6. Which of the three owns 4 changes from brick to brick. Blocks 0 and 191 touch brick 0.
All inputs are finite; a program needn't handle non-finite values.
Results may differ from the reference program's by a relative error of at most 0.00041.
Values may be sent and summed in bfloat16 or wider, within the bound.
A program may use at most 128 MiB of HBM per device.

```python
import math
import jax
import jax.numpy as jnp
from jax import lax

FB = 128
KB = 8
CAP = 4
BLK_DEV = 6
SIDE = 16
BR_DEV = 1
NF = 24576
N_DEV = 32


def draw_density_rows(key, part):
    row_count = N_DEV * BLK_DEV * FB
    col_count = 5 * BLK_DEV * FB
    row_index = jnp.arange(row_count, dtype=jnp.int32)[:, None]
    col_index = jnp.arange(col_count, dtype=jnp.int32)[None, :]
    owner_dev = (row_index // (BLK_DEV * FB)).astype(jnp.float32)
    growth = 1.0 + 2.0 * owner_dev / (N_DEV - 1)
    on_diagonal = col_index == 2 * BLK_DEV * FB + row_index % (BLK_DEV * FB)
    random_part = jnp.clip(jax.random.normal(key, (row_count, col_count), jnp.float32), -6.0, 6.0)
    values = (0.2 * random_part + 2.0 * growth * on_diagonal.astype(jnp.float32)) / (KB * FB)
    return values.astype(jnp.bfloat16)


def draw_brick_blocks(key, part):
    base_key = jax.random.fold_in(key, 11)

    def one_brick(brick):
        brick_key = jax.random.fold_in(base_key, brick)
        device = brick // BR_DEV
        heavy_side = jax.random.randint(jax.random.fold_in(brick_key, 7), (), 0, 3)
        counts = jnp.where(jnp.arange(3) == heavy_side, CAP, (KB - CAP) // 2)
        owners = jnp.mod(device + jnp.arange(3) - 1, N_DEV)
        shuffled_list = []
        for side in range(3):
            perm = jax.random.permutation(jax.random.fold_in(brick_key, side), BLK_DEV).astype(jnp.int32)
            target = jnp.where(owners[side] == 0, 0, jnp.where(owners[side] == N_DEV - 1, BLK_DEV - 1, -1))
            found = (perm == target).astype(jnp.int32)
            position = jnp.sum(found * jnp.arange(BLK_DEV, dtype=jnp.int32))
            rolled = perm[jnp.mod(jnp.arange(BLK_DEV, dtype=jnp.int32) + position, BLK_DEV)]
            use_roll = (brick == 0) & (target >= 0)
            shuffled_list.append(jnp.where(use_roll, rolled, perm))
        shuffled = jnp.stack(shuffled_list)
        chosen = jnp.arange(BLK_DEV)[None, :] < counts[:, None]
        ordering = jnp.argsort(jnp.where(chosen, 0, 1).reshape(-1), stable=True)[:KB]
        blocks = (owners[:, None] * BLK_DEV + shuffled).reshape(-1)
        return blocks[ordering].astype(jnp.int32)
    return lax.map(one_brick, jnp.arange(N_DEV * BR_DEV, dtype=jnp.int32))


def setup_inputs(seed: int = 0) -> dict:
    key_of = jax.random.split(jax.random.key(seed), 7)
    return {
        "density_rows": draw_density_rows(jax.random.fold_in(key_of[6], 71), 0),
        "center_x": jnp.clip(jax.random.uniform(key_of[1], (NF,), jnp.float32, -0.25, 1.25), -0.25, 1.25),
        "center_y": jnp.clip(jax.random.uniform(key_of[2], (NF,), jnp.float32, 0.0, 1.0), 0.0, 1.0),
        "center_z": jnp.clip(jax.random.uniform(key_of[3], (NF,), jnp.float32, 0.0, 1.0), 0.0, 1.0),
        "exponent": jnp.clip(jnp.exp(jax.random.uniform(key_of[4], (NF,), jnp.float32, math.log(0.5), math.log(150.0))), 0.5, 150.0),
        "brick_blocks": draw_brick_blocks(jax.random.fold_in(key_of[6], 71), 0),
    }


omega = 2.0 / 3.0
four_pi = 4.0 * math.pi
slater = (3.0 / math.pi) ** (1.0 / 3.0)


def periodic(distance, period):
    return jnp.mod(distance + 0.5 * period, period) - 0.5 * period


def basis_values(device, z_slot, blocks, center_x, center_y, center_z, exponent, devices):
    functions = (blocks[:, None] * FB + jnp.arange(FB, dtype=jnp.int32)[None, :]).reshape(-1)
    owner_dev = functions // (BLK_DEV * FB)
    offset = (jnp.mod(device - owner_dev + 1, devices) - 1).astype(jnp.float32)
    grid_points = (jnp.arange(SIDE, dtype=jnp.float32) + 0.5) / SIDE
    decay_rate = exponent[functions][:, None]
    along_x = offset[:, None] + grid_points[None, :] - center_x[functions][:, None]
    along_y = periodic(grid_points[None, :] - center_y[functions][:, None], 1.0)
    along_z = periodic(z_slot + grid_points[None, :] - center_z[functions][:, None], 1.0 * BR_DEV)
    factor_x = jnp.exp(-decay_rate * along_x * along_x)
    factor_y = jnp.exp(-decay_rate * along_y * along_y)
    factor_z = jnp.exp(-decay_rate * along_z * along_z)
    values = factor_x[:, :, None, None] * factor_y[:, None, :, None] * factor_z[:, None, None, :]
    return values.reshape(functions.shape[0], SIDE * SIDE * SIDE).astype(jnp.bfloat16)


def reference(density_rows, center_x, center_y, center_z, exponent, brick_blocks):
    nbricks = N_DEV * BR_DEV
    cells = SIDE * SIDE * SIDE
    density_tiles = density_rows.reshape(N_DEV * BLK_DEV, FB, 5 * BLK_DEV, FB)

    def layout(brick):
        blocks = brick_blocks[brick]
        owner_dev = blocks // BLK_DEV
        col_blocks = jnp.mod(owner_dev[None, :] - owner_dev[:, None] + 2, N_DEV) * BLK_DEV + (blocks % BLK_DEV)[None, :]
        orbitals = basis_values((brick // BR_DEV).astype(jnp.int32), (brick % BR_DEV).astype(jnp.float32), blocks,
                                center_x, center_y, center_z, exponent, N_DEV)
        return blocks, col_blocks, orbitals

    def one_density(brick):
        blocks, col_blocks, orbitals = layout(brick)
        pieces = density_tiles[blocks[:, None], :, col_blocks, :]
        matrix = pieces.transpose(0, 2, 1, 3).reshape(KB * FB, KB * FB)
        applied = jnp.dot(matrix, orbitals, preferred_element_type=jnp.float32)
        return jnp.sum(orbitals.astype(jnp.float32) * applied, axis=0)

    density = lax.map(one_density, jnp.arange(nbricks, dtype=jnp.int32))
    average = jnp.sum(density) / (nbricks * cells)
    source = density - average
    sweep_one = (omega * four_pi / 6.0) * source
    grid_field = sweep_one.reshape(N_DEV, BR_DEV, SIDE, SIDE, SIDE).transpose(0, 2, 3, 1, 4)
    grid_field = grid_field.reshape(N_DEV * SIDE, SIDE, BR_DEV * SIDE)
    beside_all = jnp.roll(grid_field, 1, 0) + jnp.roll(grid_field, -1, 0)
    beside_all = beside_all + jnp.roll(grid_field, 1, 1) + jnp.roll(grid_field, -1, 1)
    beside_all = beside_all + jnp.roll(grid_field, 1, 2) + jnp.roll(grid_field, -1, 2)
    beside_all = beside_all.reshape(N_DEV, SIDE, SIDE, BR_DEV, SIDE).transpose(0, 3, 1, 2, 4).reshape(nbricks, cells)
    sweep_two = sweep_one + omega * ((four_pi * source + beside_all) / 6.0 - sweep_one)
    potential = sweep_two - slater * jnp.cbrt(density)

    def add_brick(ham_tiles, brick):
        blocks, col_blocks, orbitals = layout(brick)
        weighted = (orbitals.astype(jnp.float32) * potential[brick][None, :]).astype(jnp.bfloat16)
        ham_brick = jnp.dot(weighted, orbitals.T, preferred_element_type=jnp.float32) * (64.0 / cells)
        pieces = ham_brick.reshape(KB, FB, KB, FB).transpose(0, 2, 1, 3)
        return ham_tiles.at[blocks[:, None], :, col_blocks, :].add(pieces), None

    start = jnp.zeros((N_DEV * BLK_DEV, FB, 5 * BLK_DEV, FB), jnp.float32)
    ham_tiles, ignored = lax.scan(add_brick, start, jnp.arange(nbricks, dtype=jnp.int32))
    return potential, ham_tiles.reshape(N_DEV * BLK_DEV * FB, 5 * BLK_DEV * FB)
```

```python
import functools
import math

import jax
import jax.numpy as jnp
from jax import lax
from jax.experimental import pallas as pl
from jax.experimental.pallas import tpu as pltpu
from jax.sharding import PartitionSpec as P

FB = 128
KB = 8
CAP = 4
BLK_DEV = 6
SIDE = 16
LAYER = SIDE * SIDE
CELLS = SIDE * SIDE * SIDE
COLS = 5 * BLK_DEV * FB
ROWS = BLK_DEV * FB
HALF = 64
VMEM_BYTES = 60 * 1024 * 1024

omega = 2.0 / 3.0
four_pi = 4.0 * math.pi
slater = (3.0 / math.pi) ** (1.0 / 3.0)
f32 = jnp.float32
bf16 = jnp.bfloat16


def wrapped(distance):
    moved = distance + 0.5
    return (moved - jnp.floor(moved)) - 0.5


def fill_orbitals(brick, devices, bb_ref, param_refs, rows_ref, orb_ref):
    point = (lax.broadcasted_iota(jnp.int32, (HALF, SIDE), 1).astype(f32) + 0.5) / SIDE
    cell = lax.broadcasted_iota(jnp.int32, (HALF, LAYER), 1)
    point_y = ((cell // SIDE).astype(f32) + 0.5) / SIDE
    point_z = ((cell % SIDE).astype(f32) + 0.5) / SIDE

    def one_block(a, carry):
        block = bb_ref[brick, a]
        owner = block // BLK_DEV
        offset = (lax.rem(brick - owner + 1 + devices, devices) - 1).astype(f32)
        for p, ref in enumerate(param_refs):
            rows_ref[p : p + 1, :] = ref[pl.ds(block, 1), :]
        turned = rows_ref[...].T
        for h in range(FB // HALF):
            part = turned[h * HALF : (h + 1) * HALF]
            rate = -part[:, 3:4]
            along_x = (offset + point) - part[:, 0:1]
            along_y = wrapped(point_y - part[:, 1:2])
            along_z = wrapped(point_z - part[:, 2:3])
            factor_x = jnp.exp(rate * along_x * along_x)
            factor_yz = jnp.exp(rate * along_y * along_y) * jnp.exp(rate * along_z * along_z)
            start = pl.multiple_of(a * FB + h * HALF, HALF)
            for i in range(SIDE):
                orb_ref[pl.ds(start, HALF), i * LAYER : (i + 1) * LAYER] = (
                    factor_x[:, i : i + 1] * factor_yz
                ).astype(bf16)
        return carry

    lax.fori_loop(0, KB, one_block, 0)


def find_slots(brick, me, bb_ref, sel_ref):
    for k in range(CAP):
        sel_ref[k] = 0
    count = jnp.int32(0)
    for a in range(KB):
        mine = bb_ref[brick, a] // BLK_DEV == me

        @pl.when(mine)
        def _():
            sel_ref[count] = a

        count = count + mine.astype(jnp.int32)
    return count


def column_block(brick, c, me, devices, bb_ref):
    block = bb_ref[brick, c]
    owner = block // BLK_DEV
    return lax.rem(owner - me + 2 + devices, devices) * BLK_DEV + (block - owner * BLK_DEV)


def row_block(brick, slot, bb_ref):
    return lax.rem(bb_ref[brick, slot], BLK_DEV)


def density_kernel(
    devices, bb_ref, rows_hbm, cx, cy, cz, ex, pd_ref, sum_ref, rows_vmem, orb_ref, mat_ref, tmp_ref, sel_ref, sem
):
    me = lax.axis_index("dev")
    load = pltpu.make_async_copy(rows_hbm, rows_vmem, sem)
    load.start()
    tmp_ref[...] = jnp.zeros_like(tmp_ref)

    def one_brick(t, carry):
        brick = lax.rem(me + t - 1 + devices, devices)
        fill_orbitals(brick, devices, bb_ref, (cx, cy, cz, ex), tmp_ref, orb_ref)
        count = find_slots(brick, me, bb_ref, sel_ref)

        @pl.when(t == 0)
        def _():
            load.wait()

        for k in range(CAP):
            here = pl.ds(k * FB, FB)

            @pl.when(k < count)
            def _():
                row = pl.multiple_of(row_block(brick, sel_ref[k], bb_ref) * FB, FB)
                for c in range(KB):
                    col = pl.multiple_of(column_block(brick, c, me, devices, bb_ref) * FB, FB)
                    mat_ref[here, c * FB : (c + 1) * FB] = rows_vmem[pl.ds(row, FB), pl.ds(col, FB)]

            @pl.when(k >= count)
            def _():
                mat_ref[here, :] = jnp.zeros((FB, KB * FB), bf16)

        def one_chunk(j, inner):
            chunk = pl.ds(pl.multiple_of(j * 2 * LAYER, 2 * LAYER), 2 * LAYER)
            applied = jnp.dot(mat_ref[...], orb_ref[:, chunk], preferred_element_type=f32)
            total = jnp.zeros((1, 2 * LAYER), f32)
            for k in range(CAP):
                row = pl.multiple_of(sel_ref[k] * FB, FB)
                own = orb_ref[pl.ds(row, FB), chunk].astype(f32)
                total = total + jnp.sum(own * applied[k * FB : (k + 1) * FB], axis=0, keepdims=True)
            pd_ref[t, pl.ds(2 * j, 1), :] = total[:, :LAYER]
            pd_ref[t, pl.ds(2 * j + 1, 1), :] = total[:, LAYER:]
            return inner

        lax.fori_loop(0, SIDE // 2, one_chunk, 0)
        return carry

    lax.fori_loop(0, 3, one_brick, 0)
    layer = jnp.sum(pd_ref[0] + pd_ref[1] + pd_ref[2], axis=0, keepdims=True)
    sum_ref[0] = layer[:, :FB] + layer[:, FB:]


def potential_kernel(
    devices, pd_ref, sum_ref, out_ref, left1, right1, left2, right2, left3, right3, sums, send_sem, recv_sem, all_sem
):
    me = lax.axis_index("dev")
    barrier = pltpu.get_barrier_semaphore()

    def at(step):
        return lax.rem(me + step + devices, devices)

    def greet(k, carry):
        pl.semaphore_signal(
            barrier, inc=1, device_id=(lax.rem(me + k, devices),), device_id_type=pl.DeviceIdType.MESH
        )
        return carry

    lax.fori_loop(1, devices, greet, 0)
    pl.semaphore_wait(barrier, devices - 1)

    def to_all(k):
        return pltpu.make_async_remote_copy(
            src_ref=sum_ref.at[0],
            dst_ref=sums.at[k - 1],
            send_sem=all_sem.at[0],
            recv_sem=all_sem.at[1],
            device_id=(lax.rem(me + k, devices),),
            device_id_type=pl.DeviceIdType.MESH,
        )

    def start_sum(k, carry):
        to_all(k).start()
        return carry

    plan = (
        (pd_ref, left1, 1),
        (pd_ref, right1, -1),
        (pd_ref.at[pl.ds(1, 2)], left2, 2),
        (pd_ref.at[pl.ds(0, 2)], right2, -2),
        (pd_ref.at[2, pl.ds(8, 8)], left3, 3),
        (pd_ref.at[0, pl.ds(0, 8)], right3, -3),
    )
    copies = [
        pltpu.make_async_remote_copy(
            src_ref=src,
            dst_ref=dst,
            send_sem=send_sem.at[q],
            recv_sem=recv_sem.at[q],
            device_id=(at(step),),
            device_id_type=pl.DeviceIdType.MESH,
        )
        for q, (src, dst, step) in enumerate(plan)
    ]
    lax.fori_loop(1, devices, start_sum, 0)
    for copy in copies:
        copy.start()
    for copy in copies:
        copy.wait()
    pltpu.make_async_copy(sums, sums, all_sem.at[0]).wait()
    pltpu.make_async_copy(sums, sums, all_sem.at[1]).wait()

    total = jnp.sum(sums[...], axis=0) + sum_ref[0]
    average = jnp.sum(total, axis=1, keepdims=True) / (devices * CELLS)
    scale = omega * four_pi / 6.0
    here = pd_ref[1] + left1[2] + right1[0]
    behind = left1[1] + left2[1] + pd_ref[0]
    ahead = right1[1] + right2[0] + pd_ref[2]
    far_behind = (left2[0, 8:] + left3[...] + left1[0, 8:])[7:]
    far_ahead = (right2[1, :8] + right3[...] + right1[2, :8])[:1]
    lane = lax.broadcasted_iota(jnp.int32, (SIDE, LAYER), 1) % SIDE
    row = lax.broadcasted_iota(jnp.int32, (SIDE, LAYER), 0)
    cases = (
        (behind, far_behind, here[:1]),
        (here, behind[SIDE - 1 :], ahead[:1]),
        (ahead, here[SIDE - 1 :], far_ahead),
    )

    def moved(x, steps, axis):
        return pltpu.roll(x, steps % x.shape[axis], axis)

    for t, (density, before, after) in enumerate(cases):
        source = density - average
        one = scale * source
        up = jnp.where(row == 0, scale * (before - average), moved(one, 1, 0))
        down = jnp.where(row == SIDE - 1, scale * (after - average), moved(one, -1, 0))
        beside = up + down + moved(one, SIDE, 1) + moved(one, -SIDE, 1)
        beside = beside + jnp.where(lane == 0, moved(one, 1 - SIDE, 1), moved(one, 1, 1))
        beside = beside + jnp.where(lane == SIDE - 1, moved(one, SIDE - 1, 1), moved(one, -1, 1))
        two = one + omega * ((four_pi * source + beside) / 6.0 - one)
        size = jnp.abs(density)
        safe = jnp.where(size > 0.0, size, 1.0)
        root = jnp.exp(jnp.log(safe) / 3.0)
        root = root - (root - safe / (root * root)) / 3.0
        root = jnp.where(size > 0.0, root, 0.0)
        root = jnp.where(density < 0.0, -root, root)
        out_ref[t] = two - slater * root


def ham_kernel(devices, bb_ref, pot_ref, cx, cy, cz, ex, out_hbm, acc_ref, orb_ref, wei_ref, tmp_ref, sel_ref, sem):
    me = lax.axis_index("dev")
    tmp_ref[...] = jnp.zeros_like(tmp_ref)

    def clear(r, carry):
        acc_ref[pl.ds(pl.multiple_of(r * 64, 64), 64), :] = jnp.zeros((64, COLS), f32)
        return carry

    lax.fori_loop(0, ROWS // 64, clear, 0)

    def one_brick(t, carry):
        brick = lax.rem(me + t - 1 + devices, devices)
        fill_orbitals(brick, devices, bb_ref, (cx, cy, cz, ex), tmp_ref, orb_ref)
        count = find_slots(brick, me, bb_ref, sel_ref)

        def weigh(k, inner):
            source = pl.multiple_of(sel_ref[k] * FB, FB)
            target = pl.multiple_of(k * FB, FB)
            for i in range(SIDE):
                cells = slice(i * LAYER, (i + 1) * LAYER)
                wei_ref[pl.ds(target, FB), cells] = (
                    orb_ref[pl.ds(source, FB), cells].astype(f32) * pot_ref[t, i : i + 1, :]
                ).astype(bf16)
            return inner

        lax.fori_loop(0, CAP, weigh, 0)

        def one_pair(q, inner):
            part = orb_ref[pl.ds(pl.multiple_of(q * 2 * FB, 2 * FB), 2 * FB), :]
            tile = lax.dot_general(
                wei_ref[...], part, (((1,), (1,)), ((), ())), preferred_element_type=f32
            ) * (64.0 / CELLS)
            for k in range(CAP):

                @pl.when(k < count)
                def _():
                    row = pl.multiple_of(row_block(brick, sel_ref[k], bb_ref) * FB, FB)
                    for c in range(2):
                        col = pl.multiple_of(column_block(brick, 2 * q + c, me, devices, bb_ref) * FB, FB)
                        acc_ref[pl.ds(row, FB), pl.ds(col, FB)] += tile[
                            k * FB : (k + 1) * FB, c * FB : (c + 1) * FB
                        ]

            return inner

        lax.fori_loop(0, KB // 2, one_pair, 0)
        return carry

    lax.fori_loop(0, 3, one_brick, 0)
    store = pltpu.make_async_copy(acc_ref, out_hbm, sem)
    store.start()
    store.wait()


def local(devices, density_rows, center_x, center_y, center_z, exponent, brick_blocks):
    params = [x.reshape(-1, FB) for x in (center_x, center_y, center_z, exponent)]
    vmem = pl.BlockSpec(memory_space=pltpu.VMEM)
    smem = pl.BlockSpec(memory_space=pltpu.SMEM)
    anywhere = pl.BlockSpec(memory_space=pl.ANY)
    grid = (3, SIDE, LAYER)
    partial, sums = pl.pallas_call(
        functools.partial(density_kernel, devices),
        out_shape=(jax.ShapeDtypeStruct(grid, f32), jax.ShapeDtypeStruct((1, 1, FB), f32)),
        in_specs=[smem, anywhere] + [vmem] * 4,
        out_specs=(vmem, vmem),
        scratch_shapes=[
            pltpu.VMEM((ROWS, COLS), bf16),
            pltpu.VMEM((KB * FB, CELLS), bf16),
            pltpu.VMEM((CAP * FB, KB * FB), bf16),
            pltpu.VMEM((8, FB), f32),
            pltpu.SMEM((CAP,), jnp.int32),
            pltpu.SemaphoreType.DMA,
        ],
        compiler_params=pltpu.CompilerParams(vmem_limit_bytes=VMEM_BYTES),
        name="partial_density",
    )(brick_blocks, density_rows, *params)
    potentials = pl.pallas_call(
        functools.partial(potential_kernel, devices),
        out_shape=jax.ShapeDtypeStruct(grid, f32),
        in_specs=[vmem, vmem],
        out_specs=vmem,
        scratch_shapes=[
            pltpu.VMEM((3, SIDE, LAYER), f32),
            pltpu.VMEM((3, SIDE, LAYER), f32),
            pltpu.VMEM((2, SIDE, LAYER), f32),
            pltpu.VMEM((2, SIDE, LAYER), f32),
            pltpu.VMEM((8, LAYER), f32),
            pltpu.VMEM((8, LAYER), f32),
            pltpu.VMEM((devices - 1, 1, FB), f32),
            pltpu.SemaphoreType.DMA((6,)),
            pltpu.SemaphoreType.DMA((6,)),
            pltpu.SemaphoreType.DMA((2,)),
        ],
        compiler_params=pltpu.CompilerParams(collective_id=0, has_side_effects=True),
        name="exchange_potential",
    )(partial, sums)
    ham = pl.pallas_call(
        functools.partial(ham_kernel, devices),
        out_shape=jax.ShapeDtypeStruct((ROWS, COLS), f32),
        in_specs=[smem] + [vmem] * 5,
        out_specs=anywhere,
        scratch_shapes=[
            pltpu.VMEM((ROWS, COLS), f32),
            pltpu.VMEM((KB * FB, CELLS), bf16),
            pltpu.VMEM((CAP * FB, CELLS), bf16),
            pltpu.VMEM((8, FB), f32),
            pltpu.SMEM((CAP,), jnp.int32),
            pltpu.SemaphoreType.DMA,
        ],
        compiler_params=pltpu.CompilerParams(vmem_limit_bytes=VMEM_BYTES),
        name="ham_rows",
    )(brick_blocks, potentials, *params)
    return potentials[1].reshape(1, CELLS), ham


def solution(mesh):
    placed = (P("dev", None), P(), P(), P(), P(), P())
    return jax.shard_map(
        functools.partial(local, mesh.shape["dev"]),
        mesh=mesh,
        in_specs=placed,
        out_specs=(P("dev", None), P("dev", None)),
        check_vma=False,
    )
```

```python
import functools
import math

import jax
import jax.numpy as jnp
from jax import lax
from jax.experimental import pallas as pl
from jax.experimental.pallas import tpu as pltpu
from jax.sharding import PartitionSpec as P

FB = 128
KB = 8
CAP = 4
BLK_DEV = 6
SIDE = 16
LAYER = SIDE * SIDE
CELLS = SIDE * SIDE * SIDE
COLS = 5 * BLK_DEV * FB
ROWS = BLK_DEV * FB
HALF = 64
VMEM_BYTES = 60 * 1024 * 1024

omega = 2.0 / 3.0
four_pi = 4.0 * math.pi
slater = (3.0 / math.pi) ** (1.0 / 3.0)
f32 = jnp.float32
bf16 = jnp.bfloat16


def wrapped(distance):
    moved = distance + 0.5
    return (moved - jnp.floor(moved)) - 0.5


def fill_orbitals(brick, devices, bb_ref, param_refs, rows_ref, orb_ref):
    point = (lax.broadcasted_iota(jnp.int32, (SIDE, FB), 0).astype(f32) + 0.5) / SIDE

    def one_block(a, carry):
        block = bb_ref[brick, a]
        owner = block // BLK_DEV
        offset = (lax.rem(brick - owner + 1 + devices, devices) - 1).astype(f32)
        mid_x, mid_y, mid_z, rate = [ref[pl.ds(block, 1), :] for ref in param_refs]
        rate = -rate
        along_x = (offset + point) - mid_x
        along_y = wrapped(point - mid_y)
        along_z = wrapped(point - mid_z)
        factor_x = jnp.exp(rate * along_x * along_x).T
        factor_y = jnp.exp(rate * along_y * along_y)
        factor_z = jnp.exp(rate * along_z * along_z)
        for j in range(SIDE):
            rows_ref[j * SIDE : (j + 1) * SIDE, :] = factor_y[j : j + 1] * factor_z
        factor_yz = rows_ref[...].T
        for h in range(FB // HALF):
            part = slice(h * HALF, (h + 1) * HALF)
            start = pl.multiple_of(a * FB + h * HALF, HALF)
            for i in range(SIDE):
                orb_ref[pl.ds(start, HALF), i * LAYER : (i + 1) * LAYER] = (
                    factor_x[part, i : i + 1] * factor_yz[part]
                ).astype(bf16)
        return carry

    lax.fori_loop(0, KB, one_block, 0)


def find_slots(brick, me, bb_ref, sel_ref):
    for k in range(CAP):
        sel_ref[k] = 0
    count = jnp.int32(0)
    for a in range(KB):
        mine = bb_ref[brick, a] // BLK_DEV == me

        @pl.when(mine)
        def _():
            sel_ref[count] = a

        count = count + mine.astype(jnp.int32)
    return count


def column_block(brick, c, me, devices, bb_ref):
    block = bb_ref[brick, c]
    owner = block // BLK_DEV
    return lax.rem(owner - me + 2 + devices, devices) * BLK_DEV + (block - owner * BLK_DEV)


def row_block(brick, slot, bb_ref):
    return lax.rem(bb_ref[brick, slot], BLK_DEV)


def density_kernel(
    devices,
    bb_ref,
    rows_hbm,
    cx,
    cy,
    cz,
    ex,
    pd_ref,
    sum_ref,
    orb_hbm,
    rows_vmem,
    orb_all,
    mat_ref,
    tmp_ref,
    sel_ref,
    sem,
    orb_sem,
):
    me = lax.axis_index("dev")
    load = pltpu.make_async_copy(rows_hbm, rows_vmem, sem)
    load.start()

    def keep(t):
        return pltpu.make_async_copy(orb_all.at[t], orb_hbm.at[t], orb_sem.at[t])

    def one_brick(t, carry):
        brick = lax.rem(me + t - 1 + devices, devices)
        orb_ref = orb_all.at[t]
        fill_orbitals(brick, devices, bb_ref, (cx, cy, cz, ex), tmp_ref, orb_ref)
        keep(t).start()
        count = find_slots(brick, me, bb_ref, sel_ref)

        @pl.when(t == 0)
        def _():
            load.wait()

        for k in range(CAP):
            here = pl.ds(k * FB, FB)

            @pl.when(k < count)
            def _():
                row = pl.multiple_of(row_block(brick, sel_ref[k], bb_ref) * FB, FB)
                for c in range(KB):
                    col = pl.multiple_of(column_block(brick, c, me, devices, bb_ref) * FB, FB)
                    mat_ref[here, c * FB : (c + 1) * FB] = rows_vmem[pl.ds(row, FB), pl.ds(col, FB)]

            @pl.when(k >= count)
            def _():
                mat_ref[here, :] = jnp.zeros((FB, KB * FB), bf16)

        def one_chunk(j, inner):
            chunk = pl.ds(pl.multiple_of(j * 2 * LAYER, 2 * LAYER), 2 * LAYER)
            applied = jnp.dot(mat_ref[...], orb_ref[:, chunk], preferred_element_type=f32)
            total = jnp.zeros((1, 2 * LAYER), f32)
            for k in range(CAP):
                row = pl.multiple_of(sel_ref[k] * FB, FB)
                own = orb_ref[pl.ds(row, FB), chunk].astype(f32)
                total = total + jnp.sum(own * applied[k * FB : (k + 1) * FB], axis=0, keepdims=True)
            pd_ref[t, pl.ds(2 * j, 1), :] = total[:, :LAYER]
            pd_ref[t, pl.ds(2 * j + 1, 1), :] = total[:, LAYER:]
            return inner

        lax.fori_loop(0, SIDE // 2, one_chunk, 0)
        return carry

    lax.fori_loop(0, 3, one_brick, 0)
    layer = jnp.sum(pd_ref[0] + pd_ref[1] + pd_ref[2], axis=0, keepdims=True)
    sum_ref[0] = layer[:, :FB] + layer[:, FB:]
    for t in range(3):
        keep(t).wait()


def potential_kernel(
    devices, pd_ref, sum_ref, out_ref, left1, right1, left2, right2, left3, right3, sums, send_sem, recv_sem, all_sem
):
    me = lax.axis_index("dev")
    barrier = pltpu.get_barrier_semaphore()

    def at(step):
        return lax.rem(me + step + devices, devices)

    def greet(k, carry):
        pl.semaphore_signal(
            barrier, inc=1, device_id=(lax.rem(me + k, devices),), device_id_type=pl.DeviceIdType.MESH
        )
        return carry

    lax.fori_loop(1, devices, greet, 0)
    pl.semaphore_wait(barrier, devices - 1)

    def to_all(k):
        return pltpu.make_async_remote_copy(
            src_ref=sum_ref.at[0],
            dst_ref=sums.at[k - 1],
            send_sem=all_sem.at[0],
            recv_sem=all_sem.at[1],
            device_id=(lax.rem(me + k, devices),),
            device_id_type=pl.DeviceIdType.MESH,
        )

    def start_sum(k, carry):
        to_all(k).start()
        return carry

    plan = (
        (pd_ref, left1, 1),
        (pd_ref, right1, -1),
        (pd_ref.at[pl.ds(1, 2)], left2, 2),
        (pd_ref.at[pl.ds(0, 2)], right2, -2),
        (pd_ref.at[2, pl.ds(8, 8)], left3, 3),
        (pd_ref.at[0, pl.ds(0, 8)], right3, -3),
    )
    copies = [
        pltpu.make_async_remote_copy(
            src_ref=src,
            dst_ref=dst,
            send_sem=send_sem.at[q],
            recv_sem=recv_sem.at[q],
            device_id=(at(step),),
            device_id_type=pl.DeviceIdType.MESH,
        )
        for q, (src, dst, step) in enumerate(plan)
    ]
    lax.fori_loop(1, devices, start_sum, 0)
    for copy in copies:
        copy.start()
    for copy in copies:
        copy.wait()
    pltpu.make_async_copy(sums, sums, all_sem.at[0]).wait()
    pltpu.make_async_copy(sums, sums, all_sem.at[1]).wait()

    total = jnp.sum(sums[...], axis=0) + sum_ref[0]
    average = jnp.sum(total, axis=1, keepdims=True) / (devices * CELLS)
    scale = omega * four_pi / 6.0
    here = pd_ref[1] + left1[2] + right1[0]
    behind = left1[1] + left2[1] + pd_ref[0]
    ahead = right1[1] + right2[0] + pd_ref[2]
    far_behind = (left2[0, 8:] + left3[...] + left1[0, 8:])[7:]
    far_ahead = (right2[1, :8] + right3[...] + right1[2, :8])[:1]
    lane = lax.broadcasted_iota(jnp.int32, (SIDE, LAYER), 1) % SIDE
    row = lax.broadcasted_iota(jnp.int32, (SIDE, LAYER), 0)
    cases = (
        (behind, far_behind, here[:1]),
        (here, behind[SIDE - 1 :], ahead[:1]),
        (ahead, here[SIDE - 1 :], far_ahead),
    )

    def moved(x, steps, axis):
        return pltpu.roll(x, steps % x.shape[axis], axis)

    for t, (density, before, after) in enumerate(cases):
        source = density - average
        one = scale * source
        up = jnp.where(row == 0, scale * (before - average), moved(one, 1, 0))
        down = jnp.where(row == SIDE - 1, scale * (after - average), moved(one, -1, 0))
        beside = up + down + moved(one, SIDE, 1) + moved(one, -SIDE, 1)
        beside = beside + jnp.where(lane == 0, moved(one, 1 - SIDE, 1), moved(one, 1, 1))
        beside = beside + jnp.where(lane == SIDE - 1, moved(one, SIDE - 1, 1), moved(one, -1, 1))
        two = one + omega * ((four_pi * source + beside) / 6.0 - one)
        size = jnp.abs(density)
        safe = jnp.where(size > 0.0, size, 1.0)
        root = jnp.exp(jnp.log(safe) / 3.0)
        root = root - (root - safe / (root * root)) / 3.0
        root = jnp.where(size > 0.0, root, 0.0)
        root = jnp.where(density < 0.0, -root, root)
        out_ref[t] = two - slater * root


def ham_kernel(devices, bb_ref, pot_ref, orb_hbm, out_hbm, acc_ref, orb_all, wei_ref, sel_ref, sem, orb_sem):
    me = lax.axis_index("dev")

    def fetch(t):
        return pltpu.make_async_copy(orb_hbm.at[t], orb_all.at[t], orb_sem.at[t])

    for t in range(3):
        fetch(t).start()

    def clear(r, carry):
        acc_ref[pl.ds(pl.multiple_of(r * 64, 64), 64), :] = jnp.zeros((64, COLS), f32)
        return carry

    lax.fori_loop(0, ROWS // 64, clear, 0)

    def one_brick(t, carry):
        brick = lax.rem(me + t - 1 + devices, devices)
        orb_ref = orb_all.at[t]
        count = find_slots(brick, me, bb_ref, sel_ref)
        fetch(t).wait()

        def weigh(k, inner):
            source = pl.multiple_of(sel_ref[k] * FB, FB)
            target = pl.multiple_of(k * FB, FB)
            for i in range(SIDE):
                cells = slice(i * LAYER, (i + 1) * LAYER)
                wei_ref[pl.ds(target, FB), cells] = (
                    orb_ref[pl.ds(source, FB), cells].astype(f32) * pot_ref[t, i : i + 1, :]
                ).astype(bf16)
            return inner

        lax.fori_loop(0, CAP, weigh, 0)

        def one_pair(q, inner):
            part = orb_ref[pl.ds(pl.multiple_of(q * 2 * FB, 2 * FB), 2 * FB), :]
            tile = lax.dot_general(
                wei_ref[...], part, (((1,), (1,)), ((), ())), preferred_element_type=f32
            ) * (64.0 / CELLS)
            for k in range(CAP):

                @pl.when(k < count)
                def _():
                    row = pl.multiple_of(row_block(brick, sel_ref[k], bb_ref) * FB, FB)
                    for c in range(2):
                        col = pl.multiple_of(column_block(brick, 2 * q + c, me, devices, bb_ref) * FB, FB)
                        acc_ref[pl.ds(row, FB), pl.ds(col, FB)] += tile[
                            k * FB : (k + 1) * FB, c * FB : (c + 1) * FB
                        ]

            return inner

        lax.fori_loop(0, KB // 2, one_pair, 0)
        return carry

    lax.fori_loop(0, 3, one_brick, 0)
    store = pltpu.make_async_copy(acc_ref, out_hbm, sem)
    store.start()
    store.wait()


def local(devices, density_rows, center_x, center_y, center_z, exponent, brick_blocks):
    params = [x.reshape(-1, FB) for x in (center_x, center_y, center_z, exponent)]
    vmem = pl.BlockSpec(memory_space=pltpu.VMEM)
    smem = pl.BlockSpec(memory_space=pltpu.SMEM)
    anywhere = pl.BlockSpec(memory_space=pl.ANY)
    grid = (3, SIDE, LAYER)
    partial, sums, orbitals = pl.pallas_call(
        functools.partial(density_kernel, devices),
        out_shape=(
            jax.ShapeDtypeStruct(grid, f32),
            jax.ShapeDtypeStruct((1, 1, FB), f32),
            jax.ShapeDtypeStruct((3, KB * FB, CELLS), bf16),
        ),
        in_specs=[smem, anywhere] + [vmem] * 4,
        out_specs=(vmem, vmem, anywhere),
        scratch_shapes=[
            pltpu.VMEM((ROWS, COLS), bf16),
            pltpu.VMEM((3, KB * FB, CELLS), bf16),
            pltpu.VMEM((CAP * FB, KB * FB), bf16),
            pltpu.VMEM((LAYER, FB), f32),
            pltpu.SMEM((CAP,), jnp.int32),
            pltpu.SemaphoreType.DMA,
            pltpu.SemaphoreType.DMA((3,)),
        ],
        compiler_params=pltpu.CompilerParams(vmem_limit_bytes=VMEM_BYTES),
        name="partial_density",
    )(brick_blocks, density_rows, *params)
    potentials = pl.pallas_call(
        functools.partial(potential_kernel, devices),
        out_shape=jax.ShapeDtypeStruct(grid, f32),
        in_specs=[vmem, vmem],
        out_specs=vmem,
        scratch_shapes=[
            pltpu.VMEM((3, SIDE, LAYER), f32),
            pltpu.VMEM((3, SIDE, LAYER), f32),
            pltpu.VMEM((2, SIDE, LAYER), f32),
            pltpu.VMEM((2, SIDE, LAYER), f32),
            pltpu.VMEM((8, LAYER), f32),
            pltpu.VMEM((8, LAYER), f32),
            pltpu.VMEM((devices - 1, 1, FB), f32),
            pltpu.SemaphoreType.DMA((6,)),
            pltpu.SemaphoreType.DMA((6,)),
            pltpu.SemaphoreType.DMA((2,)),
        ],
        compiler_params=pltpu.CompilerParams(collective_id=0, has_side_effects=True),
        name="exchange_potential",
    )(partial, sums)
    ham = pl.pallas_call(
        functools.partial(ham_kernel, devices),
        out_shape=jax.ShapeDtypeStruct((ROWS, COLS), f32),
        in_specs=[smem, vmem, anywhere],
        out_specs=anywhere,
        scratch_shapes=[
            pltpu.VMEM((ROWS, COLS), f32),
            pltpu.VMEM((3, KB * FB, CELLS), bf16),
            pltpu.VMEM((CAP * FB, CELLS), bf16),
            pltpu.SMEM((CAP,), jnp.int32),
            pltpu.SemaphoreType.DMA,
            pltpu.SemaphoreType.DMA((3,)),
        ],
        compiler_params=pltpu.CompilerParams(vmem_limit_bytes=VMEM_BYTES),
        name="ham_rows",
    )(brick_blocks, potentials, orbitals)
    return potentials[1].reshape(1, CELLS), ham


def solution(mesh):
    placed = (P("dev", None), P(), P(), P(), P(), P())
    return jax.shard_map(
        functools.partial(local, mesh.shape["dev"]),
        mesh=mesh,
        in_specs=placed,
        out_specs=(P("dev", None), P("dev", None)),
        check_vma=False,
    )
```
